256 devices in a mesh: camp: 16 (over z_hi, y, core), hour: 16 (over x, z_lo).
Axes of the slice: x: 4, y: 4, z: 8 (z_hi: 2, z_lo: 4; z = z_hi * 4 + z_lo), core: 2. Of those that a mesh axis runs over, the one named last changes fastest.
Arguments:
- observed: bfloat16 [2048, 2048, 128], P('camp', 'hour'), may hold values from -6 to 6
- bucket: int32 [2048, 2048, 128], P('camp', 'hour'), may hold values from 0 to 8
- propensity: float32 [8], replicated, may hold values from 0.1 to 1
- camp_factor: float32 [2048, 256], P(('camp', 'hour')), may hold values from -2.4 to 2.4
- camp_moment: float32 [2048, 256], P(('camp', 'hour')), may hold values from -0.6 to 0.6
- camp_second: float32 [2048, 256], P(('camp', 'hour')), may hold values from 0.02 to 0.5
- hour_factor: float32 [2048, 256], P(('hour', 'camp')), may hold values from -2.4 to 2.4
- hour_moment: float32 [2048, 256], P(('hour', 'camp')), may hold values from -0.6 to 0.6
- hour_second: float32 [2048, 256], P(('hour', 'camp')), may hold values from 0.02 to 0.5
- delay_factor: float32 [128, 256], replicated, may hold values from -2.4 to 2.4
- delay_moment: float32 [128, 256], replicated, may hold values from -0.6 to 0.6
- delay_second: float32 [128, 256], replicated, may hold values from 0.02 to 0.5
Outputs:
- new_camp: float32 [2048, 256], P(('camp', 'hour'))
- new_hour: float32 [2048, 256], P(('hour', 'camp'))
- new_delay: float32 [128, 256], replicated
The draws below stay inside these ranges and needn't reach their ends.
Inputs may be any that keep to these rules, and one draw needn't show every extreme that they name: 0 marks a censored entry; bucket b of 1 to 8 takes propensity entry b - 1.
All inputs are finite; a program needn't handle non-finite values.
Results may differ from the reference program's by a relative error of at most 0.01.
Values may be sent and summed in bfloat16 or wider, within the bound.
A program may use at most 128 MiB of HBM per device.

```python
import math
import jax
import jax.numpy as jnp
from jax import lax

RANK = 256
DELAYS = 128
LEVELS = 8
STEPS = 2
CAMP_DEV = 128
CAMPAIGNS = 2048
HOURS = 2048


def touch_ends(drawn, stream_key, least, largest):
    longest = drawn.shape.index(max(drawn.shape))
    spots = []
    for shift in (0, 1):
        where = [jax.random.randint(jax.random.fold_in(stream_key, axis), (), 0, length) for axis, length in enumerate(drawn.shape)]
        where[longest] = (where[longest] + shift) % drawn.shape[longest]
        spots.append(tuple(where))
    return drawn.at[spots[0]].set(least).at[spots[1]].set(largest)


def block_levels(own_key, shape, cuts, least, largest):
    def one(axis_at, blocks):
        steps = jax.random.uniform(jax.random.fold_in(jax.random.fold_in(own_key, 6), axis_at), (blocks,), jnp.float32, least / len(cuts), largest / len(cuts))
        return jnp.repeat(jnp.exp(steps), shape[axis_at] // blocks).reshape((-1,) + (1,) * (len(shape) - axis_at - 1))

    level = one(*cuts[0])
    for cut in cuts[1:]:
        level = level * one(*cut)
    return level


def centred(rng, shape, width, bound, cuts=(), kind=jnp.bfloat16):
    entries = jax.random.normal(rng, shape, jnp.float32) * width
    if len(cuts) > 0:
        entries = block_levels(rng, shape, cuts, -0.22, 0.18) * entries
    return jnp.clip(entries, min=-bound, max=bound).astype(kind)


def setup_inputs(seed: int = 0) -> dict:
    keys = jax.random.split(jax.random.key(seed), 13)
    observed = centred(keys[0], (CAMPAIGNS, HOURS, DELAYS), 1.0, 6.0, ((0, 16), (1, 16)))
    bucket = touch_ends(jax.random.randint(keys[1], (CAMPAIGNS, HOURS, DELAYS), 0, LEVELS + 1), jax.random.fold_in(keys[1], 1), 0, LEVELS).astype(jnp.int32)
    propensity = jnp.clip(jnp.exp(jax.random.uniform(keys[2], (LEVELS,), jnp.float32, math.log(0.1), math.log(1.0))), 0.1, 1.0)
    camp_factor = centred(keys[3], (CAMPAIGNS, RANK), 0.4, 2.4, ((0, 256),), jnp.float32)
    camp_moment = centred(keys[4], (CAMPAIGNS, RANK), 0.1, 0.6, ((0, 256),), jnp.float32)
    camp_second = jnp.clip(jnp.exp(math.log(0.5) - 3.218876 * jax.random.uniform(keys[5], (CAMPAIGNS, RANK), jnp.float32) ** block_levels(keys[5], (CAMPAIGNS, RANK), ((0, 256),), -0.2, 0.2)), 0.02, 0.5)
    hour_factor = centred(keys[6], (HOURS, RANK), 0.4, 2.4, ((0, 256),), jnp.float32)
    hour_moment = centred(keys[7], (HOURS, RANK), 0.1, 0.6, ((0, 256),), jnp.float32)
    hour_second = jnp.clip(jnp.exp(math.log(0.5) - 3.218876 * jax.random.uniform(keys[8], (HOURS, RANK), jnp.float32) ** block_levels(keys[8], (HOURS, RANK), ((0, 256),), -0.2, 0.2)), 0.02, 0.5)
    delay_factor = centred(keys[9], (DELAYS, RANK), 0.4, 2.4, (), jnp.float32)
    delay_moment = centred(keys[10], (DELAYS, RANK), 0.1, 0.6, (), jnp.float32)
    delay_second = jnp.clip(jnp.exp(jax.random.uniform(keys[11], (DELAYS, RANK), jnp.float32, math.log(0.02), math.log(0.5))), 0.02, 0.5)
    return dict(observed=observed, bucket=bucket, propensity=propensity, camp_factor=camp_factor, camp_moment=camp_moment, camp_second=camp_second, hour_factor=hour_factor, hour_moment=hour_moment, hour_second=hour_second, delay_factor=delay_factor, delay_moment=delay_moment, delay_second=delay_second)


learn_rate = 0.1
beta_first = 0.9
beta_second = 0.999
adam_eps = 1e-08

def adam_update(factor, moment, second, gradient, grad_scale):
    scaled = gradient * grad_scale
    moment = beta_first * moment + (1.0 - beta_first) * scaled
    second = beta_second * second + (1.0 - beta_second) * scaled * scaled
    factor = factor - learn_rate * moment / (jnp.sqrt(second) + adam_eps)
    return (factor, moment, second)

def gradients(observed, bucket, inverse, camp_factor, hour_factor, delay_factor):
    camp_block = camp_factor.astype(jnp.bfloat16)
    hour_block = hour_factor.astype(jnp.bfloat16)
    delay_block = delay_factor.astype(jnp.bfloat16)
    khatri = (hour_block.astype(jnp.float32)[:, None, :] * delay_block.astype(jnp.float32)[None, :, :]).astype(jnp.bfloat16)
    khatri = khatri.reshape(HOURS * DELAYS, RANK)
    slabs = CAMPAIGNS // CAMP_DEV
    observed_slabs = observed.reshape(slabs, CAMP_DEV, HOURS * DELAYS)
    bucket_slabs = bucket.reshape(slabs, CAMP_DEV, HOURS * DELAYS)
    camp_slabs = camp_block.reshape(slabs, CAMP_DEV, RANK)

    def visit(totals, slab_item):
        obs_slab, bucket_slab, camp_slab = slab_item
        picked = inverse[jnp.clip(bucket_slab - 1, 0, LEVELS - 1).astype(jnp.int32)]
        weight = jnp.where(bucket_slab > 0, picked, jnp.zeros_like(picked))
        model_tile = lax.dot_general(camp_slab, khatri, (((1,), (1,)), ((), ())), preferred_element_type=jnp.float32)
        residual = (weight * (model_tile - obs_slab.astype(jnp.float32))).astype(jnp.bfloat16)
        camp_grad = jnp.dot(residual, khatri, preferred_element_type=jnp.float32)
        spread = lax.dot_general(residual, camp_slab, (((0,), (0,)), ((), ())), preferred_element_type=jnp.float32)
        spread = spread.reshape(HOURS, DELAYS, RANK)
        hour_total = totals[0] + lax.optimization_barrier(jnp.sum(spread * delay_block.astype(jnp.float32)[None, :, :], axis=1))
        delay_total = totals[1] + lax.optimization_barrier(jnp.sum(spread * hour_block.astype(jnp.float32)[:, None, :], axis=0))
        return ((hour_total, delay_total), camp_grad)
    start = (jnp.zeros((HOURS, RANK), jnp.float32), jnp.zeros((DELAYS, RANK), jnp.float32))
    (hour_grad, delay_grad), camp_grads = lax.scan(visit, start, (observed_slabs, bucket_slabs, camp_slabs))
    return (camp_grads.reshape(CAMPAIGNS, RANK), hour_grad, delay_grad)

def reference(observed, bucket, propensity, camp_factor, camp_moment, camp_second, hour_factor, hour_moment, hour_second, delay_factor, delay_moment, delay_second):
    inverse = 1.0 / propensity
    camp_scale = 1.0 / math.sqrt(HOURS * DELAYS)
    hour_scale = 1.0 / math.sqrt(CAMPAIGNS * DELAYS)
    delay_scale = 1.0 / math.sqrt(CAMPAIGNS * HOURS)
    for iteration in range(STEPS):
        camp_grad, hour_grad, delay_grad = gradients(observed, bucket, inverse, camp_factor, hour_factor, delay_factor)
        camp_factor, camp_moment, camp_second = adam_update(camp_factor, camp_moment, camp_second, camp_grad, camp_scale)
        hour_factor, hour_moment, hour_second = adam_update(hour_factor, hour_moment, hour_second, hour_grad, hour_scale)
        delay_factor, delay_moment, delay_second = adam_update(delay_factor, delay_moment, delay_second, delay_grad, delay_scale)
    return (camp_factor, hour_factor, delay_factor)
```

```python
import functools
import math

import jax
import jax.numpy as jnp
from jax import lax
from jax.experimental import pallas as pl
from jax.experimental.pallas import tpu as pltpu
from jax.sharding import PartitionSpec as P

STEPS = 2

learn_rate = 0.1
beta_first = 0.9
beta_second = 0.999
adam_eps = 1e-08

MESH = pl.DeviceIdType.MESH
f32 = jnp.float32
bf16 = jnp.bfloat16

CHUNKS = 8
ROWS_A, ROWS_B, ROWS_C, GRAD_A, GRAD_B, GRAD_C, SUM_C = range(7)
KINDS = 7


def split_sizes(camp_count, hour_count):
    high, core = 2, 2
    along_y = camp_count // (high * core)
    along_x = 4 if hour_count == 16 else 2
    return high, along_y, core, along_x, hour_count // along_x


def adam_update(factor, moment, second, gradient, grad_scale):
    scaled = gradient * grad_scale
    moment = beta_first * moment + (1.0 - beta_first) * scaled
    second = beta_second * second + (1.0 - beta_second) * scaled * scaled
    factor = factor - learn_rate * moment / (jnp.sqrt(second) + adam_eps)
    return factor, moment, second


def dot(a, b, dims):
    return lax.dot_general(a, b, (dims, ((), ())), preferred_element_type=f32)


def kernel(
    sizes,
    scales,
    obs_hbm,
    bucket_hbm,
    prop_hbm,
    *refs,
):
    state_hbm, refs = refs[:9], refs[9:]
    new_a, new_b, new_c, refs = *refs[:3], refs[3:]
    (
        obs,
        bucket,
        weight,
        prop,
        inverse,
        fa,
        ma,
        va,
        fb,
        mb,
        vb,
        fc,
        mc,
        vc,
        a_own,
        b_own,
        c_own,
        a_all,
        b_all,
        c_all,
        c_last,
        ga_out,
        gb_out,
        gc_out,
        sc_out,
        ga_in,
        gb_in,
        gc_in,
        sc_in,
        a32,
        b16,
        b32,
        c16,
        ct16,
        ga,
        gb,
        gc,
        state_sem,
        chunk_sem,
        send_sem,
        recv_sem,
    ) = refs
    high, along_y, cores, along_x, low = sizes
    n_hour, n_camp = along_x * low, high * along_y * cores
    n_xy, n_cz = along_x * along_y, cores * high * low
    scale_a, scale_b, scale_c = scales
    rows, cols, delays = obs.shape
    rank = a32.shape[1]
    part_a, part_c = rows // n_hour, delays // n_xy

    camp, hour = lax.axis_index("camp"), lax.axis_index("hour")
    z_hi, y, core = camp // (along_y * cores), (camp // cores) % along_y, camp % cores
    x, z_lo = hour // low, hour % low
    xy = x * along_y + y
    cz = (core * high + z_hi) * low + z_lo

    def hour_peer(p):
        return {"camp": camp, "hour": p}

    def camp_peer(p):
        return {"camp": p, "hour": hour}

    def xy_peer(p):
        return {"camp": (z_hi * along_y + p % along_y) * cores + core, "hour": (p // along_y) * low + z_lo}

    def cz_peer(p):
        at = (p // low) % high
        return {"camp": (at * along_y + y) * cores + p // (low * high), "hour": x * low + p % low}

    by_hour = (n_hour, hour, hour_peer)
    by_camp = (n_camp, camp, camp_peer)
    by_xy = (n_xy, xy, xy_peer)
    by_cz = (n_cz, cz, cz_peer)
    groups = (by_hour, by_camp, by_xy, by_cz)

    states = (fa, ma, va, fb, mb, vb, fc, mc, vc)
    loads = [pltpu.make_async_copy(h, v, state_sem.at[i]) for i, (h, v) in enumerate(zip(state_hbm, states))]
    loads.append(pltpu.make_async_copy(prop_hbm, prop, state_sem.at[9]))
    for load in loads:
        load.start()
    chunk = rows // CHUNKS

    def chunks_of(source, target, row):
        ats = [pl.ds(n * chunk, chunk) for n in range(CHUNKS)]
        return [pltpu.make_async_copy(source.at[at], target.at[at], chunk_sem.at[row, n]) for n, at in enumerate(ats)]

    bucket_chunks, obs_chunks = chunks_of(bucket_hbm, bucket, 0), chunks_of(obs_hbm, obs, 1)
    for load in bucket_chunks + obs_chunks:
        load.start()

    barrier = pltpu.get_barrier_semaphore()
    for size, me, peer in groups:

        def greet(t, _, size=size, me=me, peer=peer):
            pl.semaphore_signal(barrier, inc=1, device_id=peer((me + t) % size), device_id_type=MESH)
            return 0

        lax.fori_loop(1, size, greet, 0)
    pl.semaphore_wait(barrier, sum(size - 1 for size, _, _ in groups))

    def send(src, dst, step, kind, device):
        pltpu.make_async_remote_copy(
            src_ref=src,
            dst_ref=dst,
            send_sem=send_sem.at[step, kind],
            recv_sem=recv_sem.at[step, kind],
            device_id=device,
            device_id_type=MESH,
        ).start()

    def to_each(group, src, dst, step, kind):
        size, me, peer = group

        def one(t, _):
            p = (me + t) % size
            block = src.at[step] if len(src.shape) == len(dst.shape) - 1 else src.at[step, p]
            send(block, dst.at[step, me], step, kind, peer(p))
            return 0

        lax.fori_loop(1, size, one, 0)

    def arrived(size, dst, step, kind):
        got = dst.at[step, pl.ds(0, size - 1)]
        pltpu.make_async_copy(got, got, recv_sem.at[step, kind]).wait()

    def total(buf, step, size):
        out = buf[step, 0].astype(f32)
        for p in range(1, size):
            out = out + buf[step, p].astype(f32)
        return out

    def give(own, everyone, group, value, step, kind):
        own[step] = value
        everyone[step, group[1]] = value
        to_each(group, own, everyone, step, kind)

    for load in loads:
        load.wait()
    give(a_own, a_all, by_hour, fa[...].astype(bf16), 0, ROWS_A)
    give(b_own, b_all, by_camp, fb[...].astype(bf16), 0, ROWS_B)

    for level in range(prop.shape[0]):
        inverse[level] = 1.0 / jnp.full((8, delays), prop[level], f32)

    def weigh(i, _):
        b = bucket[i].reshape(cols // 8, 8, delays)

        def inv(level):
            return jnp.broadcast_to(inverse[level][None], b.shape)

        one, two, four = (b & 1) != 0, (b & 2) != 0, (b & 4) != 0
        last = jnp.where(b > 7, inv(7), 0.0)
        low_half = jnp.where(two, jnp.where(one, inv(2), inv(1)), jnp.where(one, inv(0), last))
        high_half = jnp.where(two, jnp.where(one, inv(6), inv(5)), jnp.where(one, inv(4), inv(3)))
        weight[i] = jnp.where(four, high_half, low_half).reshape(cols, delays)
        return 0

    for n in range(CHUNKS):
        bucket_chunks[n].wait()
        lax.fori_loop(n * chunk, (n + 1) * chunk, weigh, 0)
    for load in obs_chunks:
        load.wait()

    c16[...] = fc[...].astype(bf16)
    c_mine = pl.ds(pl.multiple_of(xy * part_c, 8), part_c)

    for step in range(STEPS):
        last = step == STEPS - 1
        arrived(n_hour, a_all, step, ROWS_A)
        arrived(n_camp, b_all, step, ROWS_B)
        a32[...] = a_all[step].astype(f32).reshape(rows, rank)
        b32[...] = b_all[step].astype(f32).reshape(cols, rank)
        b16[...] = b32[...].astype(bf16)
        if step > 0:
            arrived(n_xy, c_all, step - 1, ROWS_C)
            c16[...] = c_all[step - 1].astype(f32).reshape(delays, rank).astype(bf16)
        ct16[...] = c16[...].astype(f32).T.astype(bf16)
        gb[...] = jnp.zeros_like(gb)
        gc[...] = jnp.zeros_like(gc)

        def block(t, _):
            owner = (hour + 1 + t) % n_hour
            first = owner * part_a
            for half in range(part_a // 4):
                begin = first + half * 4
                pairs = jnp.concatenate([a32[pl.ds(begin + u, 1), :].astype(bf16) * b16[...] for u in range(4)], 0)
                model = dot(pairs, ct16[...], ((1,), (0,)))
                seen = obs[pl.ds(begin, 4)].reshape(4 * cols, delays).astype(f32)
                residual = (weight[pl.ds(begin, 4)].reshape(4 * cols, delays) * (model - seen)).astype(bf16)
                spread = dot(residual, c16[...], ((1,), (0,)))
                gc[...] += dot(residual, pairs, ((0,), (0,)))
                sums = gb[...]
                for u in range(4):
                    mine = spread[u * cols : (u + 1) * cols]
                    sums = sums + a32[pl.ds(begin + u, 1), :] * mine
                    ga[pl.ds(half * 4 + u, 1), :] = jnp.sum(b32[...] * mine, axis=0, keepdims=True)
                gb[...] = sums
            piece = ga[...].astype(bf16)

            @pl.when(t < n_hour - 1)
            def _():
                ga_out[step, owner] = piece
                send(ga_out.at[step, owner], ga_in.at[step, hour], step, GRAD_A, hour_peer(owner))

            @pl.when(t == n_hour - 1)
            def _():
                ga_in[step, owner] = piece

            return 0

        lax.fori_loop(0, n_hour, block, 0)

        gc_out[step] = gc[...].reshape(gc_out.shape[1:]).astype(bf16)
        gc_in[step, xy] = gc_out[step, xy]
        to_each(by_xy, gc_out, gc_in, step, GRAD_C)
        gb_out[step] = gb[...].reshape(gb_out.shape[1:]).astype(bf16)
        gb_in[step, camp] = gb_out[step, camp]
        to_each(by_camp, gb_out, gb_in, step, GRAD_B)

        arrived(n_hour, ga_in, step, GRAD_A)
        fa[...], ma[...], va[...] = adam_update(fa[...], ma[...], va[...], total(ga_in, step, n_hour), scale_a)
        if not last:
            give(a_own, a_all, by_hour, fa[...].astype(bf16), step + 1, ROWS_A)

        arrived(n_xy, gc_in, step, GRAD_C)
        give(sc_out, sc_in, by_cz, total(gc_in, step, n_xy).astype(bf16), step, SUM_C)

        arrived(n_camp, gb_in, step, GRAD_B)
        fb[...], mb[...], vb[...] = adam_update(fb[...], mb[...], vb[...], total(gb_in, step, n_camp), scale_b)
        if not last:
            give(b_own, b_all, by_camp, fb[...].astype(bf16), step + 1, ROWS_B)

        arrived(n_cz, sc_in, step, SUM_C)
        fresh = adam_update(fc[c_mine], mc[c_mine], vc[c_mine], total(sc_in, step, n_cz), scale_c)
        fc[c_mine], mc[c_mine], vc[c_mine] = fresh
        if not last:
            give(c_own, c_all, by_xy, fresh[0].astype(bf16), step, ROWS_C)
        else:
            c_last[0, xy] = fresh[0]
            size, me, peer = by_xy

            def final(t, _):
                send(c_last.at[0, me], c_last.at[0, me], step, ROWS_C, peer((me + t) % size))
                return 0

            lax.fori_loop(1, size, final, 0)
            new_a[...] = fa[...]
            new_b[...] = fb[...]
            got = c_last.at[0, pl.ds(0, n_xy - 1)]
            pltpu.make_async_copy(got, got, recv_sem.at[step, ROWS_C]).wait()
            new_c[...] = c_last[0].reshape(delays, rank)

    def sent(size, buf, step, kind):
        gone = buf.at[step, pl.ds(0, size - 1)]
        pltpu.make_async_copy(gone, gone, send_sem.at[step, kind]).wait()

    for step in range(STEPS):
        sent(n_hour, a_all, step, ROWS_A)
        sent(n_camp, b_all, step, ROWS_B)
        sent(n_hour, ga_in, step, GRAD_A)
        sent(n_camp, gb_in, step, GRAD_B)
        sent(n_xy, gc_in, step, GRAD_C)
        sent(n_cz, sc_in, step, SUM_C)
        if step < STEPS - 1:
            sent(n_xy, c_all, step, ROWS_C)
        else:
            gone = c_last.at[0, pl.ds(0, n_xy - 1)]
            pltpu.make_async_copy(gone, gone, send_sem.at[step, ROWS_C]).wait()


def body(observed, bucket, propensity, *state):
    rows, cols, delays = observed.shape
    part_a, rank = state[0].shape
    part_b = state[3].shape[0]
    n_camp, n_hour = lax.axis_size("camp"), lax.axis_size("hour")
    sizes = split_sizes(n_camp, n_hour)
    high, along_y, cores, along_x, low = sizes
    n_xy, n_cz = along_x * along_y, cores * high * low
    part_c = delays // n_xy
    scales = (
        1.0 / math.sqrt(cols * n_hour * delays),
        1.0 / math.sqrt(rows * n_camp * delays),
        1.0 / math.sqrt(rows * n_camp * cols * n_hour),
    )
    vmem = pltpu.VMEM
    scratch = [
        vmem((rows, cols, delays), bf16),
        vmem((rows, cols, delays), jnp.int32),
        vmem((rows, cols, delays), f32),
        pltpu.SMEM(propensity.shape, f32),
        vmem((propensity.shape[0], 8, delays), f32),
    ]
    scratch += [vmem(s.shape, f32) for s in state]
    scratch += [vmem((STEPS, p, rank), bf16) for p in (part_a, part_b, part_c)]
    scratch += [
        vmem((STEPS, n_hour, part_a, rank), bf16),
        vmem((STEPS, n_camp, part_b, rank), bf16),
        vmem((STEPS, n_xy, part_c, rank), bf16),
        vmem((1, n_xy, part_c, rank), f32),
        vmem((STEPS, n_hour, part_a, rank), bf16),
        vmem((STEPS, n_camp, part_b, rank), bf16),
        vmem((STEPS, n_xy, part_c, rank), bf16),
        vmem((STEPS, part_c, rank), bf16),
        vmem((STEPS, n_hour, part_a, rank), bf16),
        vmem((STEPS, n_camp, part_b, rank), bf16),
        vmem((STEPS, n_xy, part_c, rank), bf16),
        vmem((STEPS, n_cz, part_c, rank), bf16),
        vmem((rows, rank), f32),
        vmem((cols, rank), bf16),
        vmem((cols, rank), f32),
        vmem((delays, rank), bf16),
        vmem((rank, delays), bf16),
        vmem((part_a, rank), f32),
        vmem((cols, rank), f32),
        vmem((delays, rank), f32),
        pltpu.SemaphoreType.DMA((10,)),
        pltpu.SemaphoreType.DMA((2, CHUNKS)),
        pltpu.SemaphoreType.DMA((STEPS, KINDS)),
        pltpu.SemaphoreType.DMA((STEPS, KINDS)),
    ]
    anywhere, whole = pl.BlockSpec(memory_space=pltpu.HBM), pl.BlockSpec(memory_space=vmem)
    return pl.pallas_call(
        functools.partial(kernel, sizes, scales),
        out_shape=(
            jax.ShapeDtypeStruct(state[0].shape, f32),
            jax.ShapeDtypeStruct(state[3].shape, f32),
            jax.ShapeDtypeStruct(state[6].shape, f32),
        ),
        in_specs=[anywhere] * 12,
        out_specs=(whole, whole, whole),
        scratch_shapes=scratch,
        compiler_params=pltpu.CompilerParams(
            collective_id=0, has_side_effects=True, vmem_limit_bytes=67_043_328
        ),
        name="factor_steps",
    )(observed, bucket, propensity, *state)


def solution(mesh):
    rows_camp, rows_hour = P(("camp", "hour"), None), P(("hour", "camp"), None)
    in_specs = (
        P("camp", "hour", None),
        P("camp", "hour", None),
        P(),
        rows_camp,
        rows_camp,
        rows_camp,
        rows_hour,
        rows_hour,
        rows_hour,
        P(),
        P(),
        P(),
    )
    out_specs = (rows_camp, rows_hour, P())
    return jax.shard_map(body, mesh=mesh, in_specs=in_specs, out_specs=out_specs, check_vma=False)
```

```python
import functools
import math

import jax
import jax.numpy as jnp
from jax import lax
from jax.experimental import pallas as pl
from jax.experimental.pallas import tpu as pltpu
from jax.sharding import PartitionSpec as P

STEPS = 2

learn_rate = 0.1
beta_first = 0.9
beta_second = 0.999
adam_eps = 1e-08

MESH = pl.DeviceIdType.MESH
f32 = jnp.float32
bf16 = jnp.bfloat16

CHUNKS = 8
FIRST = 32
GROUP = 8
ROWS_A, ROWS_B, ROWS_C, GRAD_A, GRAD_B, GRAD_C, SUM_C = range(7)
KINDS = 7


def split_sizes(camp_count, hour_count):
    high, core = 2, 2
    along_y = camp_count // (high * core)
    along_x = 4 if hour_count == 16 else 2
    return high, along_y, core, along_x, hour_count // along_x


def adam_update(factor, moment, second, gradient, grad_scale):
    scaled = gradient * grad_scale
    moment = beta_first * moment + (1.0 - beta_first) * scaled
    second = beta_second * second + (1.0 - beta_second) * scaled * scaled
    factor = factor - learn_rate * moment / (jnp.sqrt(second) + adam_eps)
    return factor, moment, second


def dot(a, b, dims):
    return lax.dot_general(a, b, (dims, ((), ())), preferred_element_type=f32)


def kernel(
    sizes,
    scales,
    obs_hbm,
    bucket_hbm,
    prop_hbm,
    *refs,
):
    state_hbm, refs = refs[:9], refs[9:]
    new_a, new_b, new_c, refs = *refs[:3], refs[3:]
    (
        obs,
        bucket,
        weight,
        prop,
        inverse,
        resid,
        fa,
        ma,
        va,
        fb,
        mb,
        vb,
        fc,
        mc,
        vc,
        a_own,
        b_own,
        c_own,
        a_all,
        b_all,
        c_all,
        c_last,
        ga_out,
        gb_out,
        gc_out,
        sc_out,
        ga_in,
        gb_in,
        gc_in,
        sc_in,
        a32,
        b16,
        b32,
        c16,
        ct16,
        ga8,
        gc,
        state_sem,
        chunk_sem,
        send_sem,
        recv_sem,
    ) = refs
    high, along_y, cores, along_x, low = sizes
    n_hour, n_camp = along_x * low, high * along_y * cores
    n_xy, n_cz = along_x * along_y, cores * high * low
    scale_a, scale_b, scale_c = scales
    rows, cols, delays = obs.shape
    rank = a32.shape[1]
    part_b, part_c = cols // n_camp, delays // n_xy
    width = cores * part_b

    camp, hour = lax.axis_index("camp"), lax.axis_index("hour")
    div, rem = lax.div, lax.rem
    z_hi, y, core = div(camp, along_y * cores), rem(div(camp, cores), along_y), rem(camp, cores)
    x, z_lo = div(hour, low), rem(hour, low)
    xy = x * along_y + y
    cz = (core * high + z_hi) * low + z_lo

    def hour_peer(p):
        return {"camp": camp, "hour": p}

    def camp_peer(p):
        return {"camp": p, "hour": hour}

    def xy_peer(p):
        return {"camp": (z_hi * along_y + rem(p, along_y)) * cores + core, "hour": div(p, along_y) * low + z_lo}

    def cz_peer(p):
        at = rem(div(p, low), high)
        return {"camp": (at * along_y + y) * cores + div(p, low * high), "hour": x * low + rem(p, low)}

    by_hour = (n_hour, hour, hour_peer)
    by_camp = (n_camp, camp, camp_peer)
    by_xy = (n_xy, xy, xy_peer)
    by_cz = (n_cz, cz, cz_peer)
    groups = (by_hour, by_camp, by_xy, by_cz)

    states = (fa, ma, va, fb, mb, vb, fc, mc, vc)
    loads = [pltpu.make_async_copy(h, v, state_sem.at[i]) for i, (h, v) in enumerate(zip(state_hbm, states))]
    loads.append(pltpu.make_async_copy(prop_hbm, prop, state_sem.at[9]))
    for load in loads:
        load.start()
    chunk = rows // CHUNKS

    def chunks_of(source, target, row):
        ats = [pl.ds(n * chunk, chunk) for n in range(CHUNKS)]
        return [pltpu.make_async_copy(source.at[at], target.at[at], chunk_sem.at[row, n]) for n, at in enumerate(ats)]

    bucket_chunks, obs_chunks = chunks_of(bucket_hbm, bucket, 0), chunks_of(obs_hbm, obs, 1)
    for load in bucket_chunks + obs_chunks:
        load.start()

    barrier = pltpu.get_barrier_semaphore()
    for size, me, peer in groups:
        for t in range(1, size):
            pl.semaphore_signal(barrier, inc=1, device_id=peer(rem(me + t, size)), device_id_type=MESH)
    pl.semaphore_wait(barrier, sum(size - 1 for size, _, _ in groups))

    def send(src, dst, step, kind, device):
        pltpu.make_async_remote_copy(
            src_ref=src,
            dst_ref=dst,
            send_sem=send_sem.at[step, kind],
            recv_sem=recv_sem.at[step, kind],
            device_id=device,
            device_id_type=MESH,
        ).start()

    def to_each(group, src, dst, step, kind):
        size, me, peer = group
        for t in range(1, size):
            p = rem(me + t, size)
            block = src.at[step] if len(src.shape) == len(dst.shape) - 1 else src.at[step, p]
            send(block, dst.at[step, me], step, kind, peer(p))

    def arrived(size, dst, step, kind):
        got = dst.at[step, pl.ds(0, size - 1)]
        pltpu.make_async_copy(got, got, recv_sem.at[step, kind]).wait()

    def total(buf, step, size):
        out = buf[step, 0].astype(f32)
        for p in range(1, size):
            out = out + buf[step, p].astype(f32)
        return out

    def give(own, everyone, group, value, step, kind):
        own[step] = value
        everyone[step, group[1]] = value
        to_each(group, own, everyone, step, kind)

    for load in loads:
        load.wait()
    give(a_own, a_all, by_hour, fa[...].astype(bf16), 0, ROWS_A)
    give(b_own, b_all, by_camp, fb[...].astype(bf16), 0, ROWS_B)

    for level in range(prop.shape[0]):
        inverse[level] = 1.0 / jnp.full((8, delays), prop[level], f32)

    def weigh(i, _):
        b = bucket[i].reshape(cols // 8, 8, delays)

        def inv(level):
            return jnp.broadcast_to(inverse[level][None], b.shape)

        one, two, four = (b & 1) != 0, (b & 2) != 0, (b & 4) != 0
        last = jnp.where(b > 7, inv(7), 0.0)
        low_half = jnp.where(two, jnp.where(one, inv(2), inv(1)), jnp.where(one, inv(0), last))
        high_half = jnp.where(two, jnp.where(one, inv(6), inv(5)), jnp.where(one, inv(4), inv(3)))
        weight[i] = jnp.where(four, high_half, low_half).reshape(cols, delays)
        return 0

    for n in range(CHUNKS):
        bucket_chunks[n].wait()
        lax.fori_loop(n * chunk, (n + 1) * chunk, weigh, 0)
    for load in obs_chunks:
        load.wait()

    c16[...] = fc[...].astype(bf16)
    c_mine = pl.ds(pl.multiple_of(xy * part_c, 8), part_c)

    for step in range(STEPS):
        last = step == STEPS - 1
        arrived(n_hour, a_all, step, ROWS_A)
        arrived(n_camp, b_all, step, ROWS_B)
        a32[...] = a_all[step].astype(f32).reshape(rows, rank)
        b32[...] = b_all[step].astype(f32).reshape(cols, rank)
        b16[...] = b32[...].astype(bf16)
        if step > 0:
            arrived(n_xy, c_all, step - 1, ROWS_C)
            c16[...] = c_all[step - 1].astype(f32).reshape(delays, rank).astype(bf16)
        ct16[...] = c16[...].astype(f32).T.astype(bf16)
        ga8[...] = jnp.zeros_like(ga8)
        gc[...] = jnp.zeros_like(gc)

        def first_pass(g, _):
            begin = g * FIRST
            pairs, residuals = [], []
            for i in range(0, FIRST, 2):
                at = pl.ds(begin + i, 2)
                pair = jnp.concatenate([a32[pl.ds(begin + i + u, 1), :].astype(bf16) * b16[...] for u in range(2)], 0)
                model = dot(pair, ct16[...], ((1,), (0,)))
                seen = obs[at].reshape(2 * cols, delays).astype(f32)
                residual = (weight[at].reshape(2 * cols, delays) * (model - seen)).astype(bf16)
                resid[at] = residual.reshape(2, cols, delays)
                pairs.append(pair)
                residuals.append(residual)
            gc[...] += dot(jnp.concatenate(residuals, 0), jnp.concatenate(pairs, 0), ((0,), (0,)))
            return 0

        lax.fori_loop(0, rows // FIRST, first_pass, 0)
        gc_out[step] = gc[...].reshape(gc_out.shape[1:]).astype(bf16)
        gc_in[step, xy] = gc_out[step, xy]
        to_each(by_xy, gc_out, gc_in, step, GRAD_C)

        def second_pass(t, _):
            there = rem(z_hi + 1 + div(t, along_y), high) * along_y + rem(y + 1 + rem(t, along_y), along_y)
            cut = pl.multiple_of(there * width, width)
            at = pl.ds(cut, width)
            sums = [jnp.zeros((8, rank), f32) for _ in range(width // 8)]
            factor = b32[at]
            for begin in range(0, rows, GROUP):
                spread = dot(resid[pl.ds(begin, GROUP), at].reshape(GROUP * width, delays), c16[...], ((1,), (0,)))
                for u in range(GROUP):
                    row = a32[pl.ds(begin + u, 1), :]
                    part = None
                    for n in range(width // 8):
                        piece = spread[u * width + n * 8 : u * width + n * 8 + 8]
                        sums[n] = sums[n] + row * piece
                        scaled = factor[n * 8 : n * 8 + 8] * piece
                        part = scaled if part is None else part + scaled
                    ga8[begin + u] += part
            peer_rows = jnp.concatenate(sums, 0).reshape(cores, part_b, rank).astype(bf16)
            for n in range(cores):
                owner = there * cores + n

                @pl.when(owner != camp)
                def _(n=n, owner=owner):
                    gb_out[step, owner] = peer_rows[n]
                    send(gb_out.at[step, owner], gb_in.at[step, camp], step, GRAD_B, camp_peer(owner))

                @pl.when(owner == camp)
                def _(n=n, owner=owner):
                    gb_in[step, owner] = peer_rows[n]

            return 0

        lax.fori_loop(0, cols // width, second_pass, 0)
        ga_out[step] = jnp.sum(ga8[...], axis=1).reshape(ga_out.shape[1:]).astype(bf16)
        ga_in[step, hour] = ga_out[step, hour]
        to_each(by_hour, ga_out, ga_in, step, GRAD_A)

        arrived(n_xy, gc_in, step, GRAD_C)
        give(sc_out, sc_in, by_cz, total(gc_in, step, n_xy).astype(bf16), step, SUM_C)

        arrived(n_camp, gb_in, step, GRAD_B)
        fb[...], mb[...], vb[...] = adam_update(fb[...], mb[...], vb[...], total(gb_in, step, n_camp), scale_b)
        if not last:
            give(b_own, b_all, by_camp, fb[...].astype(bf16), step + 1, ROWS_B)

        arrived(n_hour, ga_in, step, GRAD_A)
        fa[...], ma[...], va[...] = adam_update(fa[...], ma[...], va[...], total(ga_in, step, n_hour), scale_a)
        if not last:
            give(a_own, a_all, by_hour, fa[...].astype(bf16), step + 1, ROWS_A)

        arrived(n_cz, sc_in, step, SUM_C)
        fresh = adam_update(fc[c_mine], mc[c_mine], vc[c_mine], total(sc_in, step, n_cz), scale_c)
        fc[c_mine], mc[c_mine], vc[c_mine] = fresh
        if not last:
            give(c_own, c_all, by_xy, fresh[0].astype(bf16), step, ROWS_C)
        else:
            c_last[0, xy] = fresh[0]
            for t in range(1, n_xy):
                send(c_last.at[0, xy], c_last.at[0, xy], step, ROWS_C, xy_peer(rem(xy + t, n_xy)))
            new_a[...] = fa[...]
            new_b[...] = fb[...]
            got = c_last.at[0, pl.ds(0, n_xy - 1)]
            pltpu.make_async_copy(got, got, recv_sem.at[step, ROWS_C]).wait()
            new_c[...] = c_last[0].reshape(delays, rank)

    def sent(size, buf, step, kind):
        gone = buf.at[step, pl.ds(0, size - 1)]
        pltpu.make_async_copy(gone, gone, send_sem.at[step, kind]).wait()

    for step in range(STEPS):
        sent(n_hour, a_all, step, ROWS_A)
        sent(n_camp, b_all, step, ROWS_B)
        sent(n_hour, ga_in, step, GRAD_A)
        sent(n_camp, gb_in, step, GRAD_B)
        sent(n_xy, gc_in, step, GRAD_C)
        sent(n_cz, sc_in, step, SUM_C)
        if step < STEPS - 1:
            sent(n_xy, c_all, step, ROWS_C)
        else:
            gone = c_last.at[0, pl.ds(0, n_xy - 1)]
            pltpu.make_async_copy(gone, gone, send_sem.at[step, ROWS_C]).wait()


def body(observed, bucket, propensity, *state):
    rows, cols, delays = observed.shape
    part_a, rank = state[0].shape
    part_b = state[3].shape[0]
    n_camp, n_hour = lax.axis_size("camp"), lax.axis_size("hour")
    sizes = split_sizes(n_camp, n_hour)
    high, along_y, cores, along_x, low = sizes
    n_xy, n_cz = along_x * along_y, cores * high * low
    part_c = delays // n_xy
    scales = (
        1.0 / math.sqrt(cols * n_hour * delays),
        1.0 / math.sqrt(rows * n_camp * delays),
        1.0 / math.sqrt(rows * n_camp * cols * n_hour),
    )
    vmem = pltpu.VMEM
    scratch = [
        vmem((rows, cols, delays), bf16),
        vmem((rows, cols, delays), jnp.int32),
        vmem((rows, cols, delays), f32),
        pltpu.SMEM(propensity.shape, f32),
        vmem((propensity.shape[0], 8, delays), f32),
        vmem((rows, cols, delays), bf16),
    ]
    scratch += [vmem(s.shape, f32) for s in state]
    scratch += [vmem((STEPS, p, rank), bf16) for p in (part_a, part_b, part_c)]
    scratch += [
        vmem((STEPS, n_hour, part_a, rank), bf16),
        vmem((STEPS, n_camp, part_b, rank), bf16),
        vmem((STEPS, n_xy, part_c, rank), bf16),
        vmem((1, n_xy, part_c, rank), f32),
        vmem((STEPS, n_hour, part_a, rank), bf16),
        vmem((STEPS, n_camp, part_b, rank), bf16),
        vmem((STEPS, n_xy, part_c, rank), bf16),
        vmem((STEPS, part_c, rank), bf16),
        vmem((STEPS, n_hour, part_a, rank), bf16),
        vmem((STEPS, n_camp, part_b, rank), bf16),
        vmem((STEPS, n_xy, part_c, rank), bf16),
        vmem((STEPS, n_cz, part_c, rank), bf16),
        vmem((rows, rank), f32),
        vmem((cols, rank), bf16),
        vmem((cols, rank), f32),
        vmem((delays, rank), bf16),
        vmem((rank, delays), bf16),
        vmem((rows, 8, rank), f32),
        vmem((delays, rank), f32),
        pltpu.SemaphoreType.DMA((10,)),
        pltpu.SemaphoreType.DMA((2, CHUNKS)),
        pltpu.SemaphoreType.DMA((STEPS, KINDS)),
        pltpu.SemaphoreType.DMA((STEPS, KINDS)),
    ]
    def finish(*refs):
        copies = [pltpu.make_async_copy(refs[i], refs[3 + i], refs[6].at[i]) for i in range(3)]
        for c in copies:
            c.start()
        for c in copies:
            c.wait()

    anywhere, whole = pl.BlockSpec(memory_space=pltpu.HBM), pl.BlockSpec(memory_space=vmem)
    made = pl.pallas_call(
        functools.partial(kernel, sizes, scales),
        out_shape=(
            vmem(state[0].shape, f32),
            vmem(state[3].shape, f32),
            vmem(state[6].shape, f32),
        ),
        in_specs=[anywhere] * 12,
        out_specs=(whole, whole, whole),
        scratch_shapes=scratch,
        compiler_params=pltpu.CompilerParams(
            collective_id=0, has_side_effects=True, vmem_limit_bytes=40 * 1024 * 1024
        ),
        name="factor_steps",
    )(*[pltpu.with_memory_space_constraint(a, pltpu.HBM) for a in (observed, bucket, propensity, *state)])
    return pl.pallas_call(
        finish,
        out_shape=tuple(jax.ShapeDtypeStruct(m.shape, f32) for m in made),
        in_specs=[pl.BlockSpec(memory_space=vmem)] * 3,
        out_specs=(pl.BlockSpec(memory_space=pl.ANY),) * 3,
        scratch_shapes=[pltpu.SemaphoreType.DMA((3,))],
        name="outputs",
    )(*[pltpu.with_memory_space_constraint(m, vmem) for m in made])


def solution(mesh):
    rows_camp, rows_hour = P(("camp", "hour"), None), P(("hour", "camp"), None)
    in_specs = (
        P("camp", "hour", None),
        P("camp", "hour", None),
        P(),
        rows_camp,
        rows_camp,
        rows_camp,
        rows_hour,
        rows_hour,
        rows_hour,
        P(),
        P(),
        P(),
    )
    out_specs = (rows_camp, rows_hour, P())
    return jax.shard_map(body, mesh=mesh, in_specs=in_specs, out_specs=out_specs, check_vma=False)
```

```python
import functools
import math

import jax
import jax.numpy as jnp
from jax import lax
from jax.experimental import pallas as pl
from jax.experimental.pallas import tpu as pltpu
from jax.sharding import PartitionSpec as P

STEPS = 2

learn_rate = 0.1
beta_first = 0.9
beta_second = 0.999
adam_eps = 1e-08

MESH = pl.DeviceIdType.MESH
f32 = jnp.float32
bf16 = jnp.bfloat16

CHUNKS = 8
FIRST = 64
GROUP = 8
ALONG_Y = 2
ROWS_A, ROWS_B, ROWS_C, GRAD_A, GRAD_B, GRAD_C, SUM_C = range(7)
KINDS = 7


def split_sizes(camp_count, hour_count):
    high, core = 2, 2
    along_y = camp_count // (high * core)
    along_x = 4 if hour_count == 16 else 2
    return high, along_y, core, along_x, hour_count // along_x


def adam_update(factor, moment, second, gradient, grad_scale):
    scaled = gradient * grad_scale
    moment = beta_first * moment + (1.0 - beta_first) * scaled
    second = beta_second * second + (1.0 - beta_second) * scaled * scaled
    factor = factor - learn_rate * moment / (jnp.sqrt(second) + adam_eps)
    return factor, moment, second


def dot(a, b, dims):
    return lax.dot_general(a, b, (dims, ((), ())), preferred_element_type=f32)


def kernel(
    sizes,
    scales,
    obs_hbm,
    bucket_hbm,
    prop_hbm,
    *refs,
):
    state_hbm, refs = refs[:9], refs[9:]
    new_a, new_b, new_c, refs = *refs[:3], refs[3:]
    (
        obs,
        bucket,
        weight,
        prop,
        inverse,
        resid,
        fa,
        ma,
        va,
        fb,
        mb,
        vb,
        fc,
        mc,
        vc,
        a_own,
        b_own,
        c_own,
        a_all,
        b_all,
        c_all,
        c_last,
        ga_out,
        gb_out,
        gc_out,
        sc_out,
        ga_in,
        gb_in,
        gc_in,
        sc_in,
        a32,
        b16,
        b32,
        c16,
        ct16,
        ga8,
        gc,
        state_sem,
        chunk_sem,
        send_sem,
        recv_sem,
    ) = refs
    high, along_y, cores, along_x, low = sizes
    n_hour, n_camp = along_x * low, high * along_y * cores
    n_xy, n_z = along_x * along_y, high * low
    n_cxy, half = cores * n_xy, a32.shape[1] // cores
    scale_a, scale_b, scale_c = scales
    rows, cols, delays = obs.shape
    rank = a32.shape[1]
    part_b, part_c = cols // n_camp, delays // n_xy
    owners = ALONG_Y * cores
    width, y_blocks = owners * part_b, along_y // ALONG_Y

    camp, hour = lax.axis_index("camp"), lax.axis_index("hour")
    div, rem = lax.div, lax.rem
    z_hi, y, core = div(camp, along_y * cores), rem(div(camp, cores), along_y), rem(camp, cores)
    x, z_lo = div(hour, low), rem(hour, low)
    xy = x * along_y + y
    cxy, z = core * n_xy + xy, z_hi * low + z_lo

    def hour_peer(p):
        return {"camp": camp, "hour": p}

    def camp_peer(p):
        return {"camp": p, "hour": hour}

    def cxy_peer(p):
        at = rem(p, n_xy)
        return {"camp": (z_hi * along_y + rem(at, along_y)) * cores + div(p, n_xy), "hour": div(at, along_y) * low + z_lo}

    def z_peer(p):
        return {"camp": (div(p, low) * along_y + y) * cores + core, "hour": x * low + rem(p, low)}

    by_hour = (n_hour, hour, hour_peer)
    by_camp = (n_camp, camp, camp_peer)
    by_cxy = (n_cxy, cxy, cxy_peer)
    by_z = (n_z, z, z_peer)
    groups = (by_camp, by_hour, by_cxy, by_z)

    barrier = pltpu.get_barrier_semaphore()
    for size, me, peer in groups:
        for t in range(1, size):
            pl.semaphore_signal(barrier, inc=1, device_id=peer(rem(me + t, size)), device_id_type=MESH)

    states = (fa, ma, va, fb, mb, vb, fc, mc, vc)
    loads = [pltpu.make_async_copy(h, v, state_sem.at[i]) for i, (h, v) in enumerate(zip(state_hbm, states))]
    loads.append(pltpu.make_async_copy(prop_hbm, prop, state_sem.at[9]))
    for load in loads:
        load.start()
    chunk = rows // CHUNKS

    def chunks_of(source, target, row):
        ats = [pl.ds(n * chunk, chunk) for n in range(CHUNKS)]
        return [pltpu.make_async_copy(source.at[at], target.at[at], chunk_sem.at[row, n]) for n, at in enumerate(ats)]

    bucket_chunks, obs_chunks = chunks_of(bucket_hbm, bucket, 0), chunks_of(obs_hbm, obs, 1)
    for load in bucket_chunks + obs_chunks:
        load.start()

    pl.semaphore_wait(barrier, sum(size - 1 for size, _, _ in groups))

    def send(src, dst, step, kind, device):
        pltpu.make_async_remote_copy(
            src_ref=src,
            dst_ref=dst,
            send_sem=send_sem.at[step, kind],
            recv_sem=recv_sem.at[step, kind],
            device_id=device,
            device_id_type=MESH,
        ).start()

    def to_each(group, src, dst, step, kind):
        size, me, peer = group
        for t in range(1, size):
            p = rem(me + t, size)
            block = src.at[step] if len(src.shape) == len(dst.shape) - 1 else src.at[step, p]
            send(block, dst.at[step, me], step, kind, peer(p))

    def arrived(size, dst, step, kind):
        got = dst.at[step, pl.ds(0, size - 1)]
        pltpu.make_async_copy(got, got, recv_sem.at[step, kind]).wait()

    def total(buf, step, size):
        out = buf[step, 0].astype(f32)
        for p in range(1, size):
            out = out + buf[step, p].astype(f32)
        return out

    def give(own, everyone, group, value, step, kind):
        own[step] = value
        everyone[step, group[1]] = value
        to_each(group, own, everyone, step, kind)

    for load in loads:
        load.wait()
    give(a_own, a_all, by_hour, fa[...].astype(bf16), 0, ROWS_A)
    give(b_own, b_all, by_camp, fb[...].astype(bf16), 0, ROWS_B)

    for level in range(prop.shape[0]):
        inverse[level] = 1.0 / jnp.full((8, delays), prop[level], f32)

    def weigh(i, _):
        b = bucket[i].reshape(cols // 8, 8, delays)

        def inv(level):
            return jnp.broadcast_to(inverse[level][None], b.shape)

        one, two, four = (b & 1) != 0, (b & 2) != 0, (b & 4) != 0
        last = jnp.where(b > 7, inv(7), 0.0)
        low_half = jnp.where(two, jnp.where(one, inv(2), inv(1)), jnp.where(one, inv(0), last))
        high_half = jnp.where(two, jnp.where(one, inv(6), inv(5)), jnp.where(one, inv(4), inv(3)))
        weight[i] = jnp.where(four, high_half, low_half).reshape(cols, delays)
        return 0

    for n in range(CHUNKS):
        bucket_chunks[n].wait()
        lax.fori_loop(n * chunk, (n + 1) * chunk, weigh, 0)
    for load in obs_chunks:
        load.wait()

    c16[...] = fc[...].astype(bf16)
    c_mine = (pl.ds(pl.multiple_of(xy * part_c, 8), part_c), pl.ds(pl.multiple_of(core * half, 128), half))

    def halves(buf):
        return [(buf.at[pl.ds(n * n_xy, n_xy)], slice(n * half, (n + 1) * half)) for n in range(cores)]


    for step in range(STEPS):
        last = step == STEPS - 1
        ga8[...] = jnp.zeros_like(ga8)
        gc[...] = jnp.zeros_like(gc)
        arrived(n_hour, a_all, step, ROWS_A)
        arrived(n_camp, b_all, step, ROWS_B)
        a32[...] = a_all[step].astype(f32).reshape(rows, rank)
        b32[...] = b_all[step].astype(f32).reshape(cols, rank)
        b16[...] = b32[...].astype(bf16)
        if step > 0:
            arrived(n_cxy, c_all, step - 1, ROWS_C)
            for blocks, ranks in halves(c_all.at[step - 1]):
                c16[:, ranks] = blocks[...].astype(f32).reshape(delays, half).astype(bf16)
        ct16[...] = c16[...].astype(f32).T.astype(bf16)

        def first_pass(g, _):
            begin = g * FIRST
            pairs, residuals = [], []
            for i in range(0, FIRST, 2):
                at = pl.ds(begin + i, 2)
                pair = jnp.concatenate([a32[pl.ds(begin + i + u, 1), :].astype(bf16) * b16[...] for u in range(2)], 0)
                model = dot(pair, ct16[...], ((1,), (0,)))
                seen = obs[at].reshape(2 * cols, delays).astype(f32)
                residual = (weight[at].reshape(2 * cols, delays) * (model - seen)).astype(bf16)
                resid[at] = residual.reshape(2, cols, delays)
                pairs.append(pair)
                residuals.append(residual)
            gc[...] += dot(jnp.concatenate(residuals, 0), jnp.concatenate(pairs, 0), ((0,), (0,)))
            return 0

        lax.fori_loop(0, rows // FIRST, first_pass, 0)
        for blocks, ranks in halves(gc_out.at[step]):
            blocks[...] = gc[:, ranks].reshape(n_xy, part_c, half).astype(bf16)
        gc_in[step, cxy] = gc_out[step, cxy]
        to_each(by_cxy, gc_out, gc_in, step, GRAD_C)

        def second_pass(t, _):
            there = rem(z_hi + 1 + div(t, y_blocks), high) * y_blocks
            there += rem(div(y, ALONG_Y) + 1 + rem(t, y_blocks), y_blocks)
            cut = pl.multiple_of(there * width, width)
            at = pl.ds(cut, width)
            sums = [jnp.zeros((8, rank), f32) for _ in range(width // 8)]
            factor = b32[at]
            for begin in range(0, rows, GROUP):
                spread = dot(resid[pl.ds(begin, GROUP), at].reshape(GROUP * width, delays), c16[...], ((1,), (0,)))
                for u in range(GROUP):
                    row = a32[pl.ds(begin + u, 1), :]
                    part = None
                    for n in range(width // 8):
                        piece = spread[u * width + n * 8 : u * width + n * 8 + 8]
                        sums[n] = sums[n] + row * piece
                        scaled = factor[n * 8 : n * 8 + 8] * piece
                        part = scaled if part is None else part + scaled
                    ga8[begin + u] += part
            peer_rows = jnp.concatenate(sums, 0).reshape(owners, part_b, rank).astype(bf16)
            for n in range(owners):
                owner = there * owners + n

                @pl.when(owner != camp)
                def _(n=n, owner=owner):
                    gb_out[step, owner] = peer_rows[n]
                    send(gb_out.at[step, owner], gb_in.at[step, camp], step, GRAD_B, camp_peer(owner))

                @pl.when(owner == camp)
                def _(n=n, owner=owner):
                    gb_in[step, owner] = peer_rows[n]

            return 0

        lax.fori_loop(0, cols // width, second_pass, 0)
        arrived(n_cxy, gc_in, step, GRAD_C)
        give(sc_out, sc_in, by_z, total(gc_in, step, n_cxy).astype(bf16), step, SUM_C)
        ga_out[step] = jnp.sum(ga8[...], axis=1).reshape(ga_out.shape[1:]).astype(bf16)
        ga_in[step, hour] = ga_out[step, hour]
        to_each(by_hour, ga_out, ga_in, step, GRAD_A)

        arrived(n_camp, gb_in, step, GRAD_B)
        fb[...], mb[...], vb[...] = adam_update(fb[...], mb[...], vb[...], total(gb_in, step, n_camp), scale_b)
        if not last:
            give(b_own, b_all, by_camp, fb[...].astype(bf16), step + 1, ROWS_B)

        arrived(n_z, sc_in, step, SUM_C)
        fresh = adam_update(fc[c_mine], mc[c_mine], vc[c_mine], total(sc_in, step, n_z), scale_c)
        fc[c_mine], mc[c_mine], vc[c_mine] = fresh
        if not last:
            give(c_own, c_all, by_cxy, fresh[0].astype(bf16), step, ROWS_C)
        else:
            c_last[0, cxy] = fresh[0]
            for t in range(1, n_cxy):
                send(c_last.at[0, cxy], c_last.at[0, cxy], step, ROWS_C, cxy_peer(rem(cxy + t, n_cxy)))

        arrived(n_hour, ga_in, step, GRAD_A)
        fa[...], ma[...], va[...] = adam_update(fa[...], ma[...], va[...], total(ga_in, step, n_hour), scale_a)
        if not last:
            give(a_own, a_all, by_hour, fa[...].astype(bf16), step + 1, ROWS_A)
        else:
            new_a[...] = fa[...]
            new_b[...] = fb[...]
            got = c_last.at[0, pl.ds(0, n_cxy - 1)]
            pltpu.make_async_copy(got, got, recv_sem.at[step, ROWS_C]).wait()
            for blocks, ranks in halves(c_last.at[0]):
                new_c[:, ranks] = blocks[...].reshape(delays, half)

    def sent(size, buf, step, kind):
        gone = buf.at[step, pl.ds(0, size - 1)]
        pltpu.make_async_copy(gone, gone, send_sem.at[step, kind]).wait()

    for step in range(STEPS):
        sent(n_hour, a_all, step, ROWS_A)
        sent(n_camp, b_all, step, ROWS_B)
        sent(n_hour, ga_in, step, GRAD_A)
        sent(n_camp, gb_in, step, GRAD_B)
        sent(n_cxy, gc_in, step, GRAD_C)
        sent(n_z, sc_in, step, SUM_C)
        if step < STEPS - 1:
            sent(n_cxy, c_all, step, ROWS_C)
        else:
            gone = c_last.at[0, pl.ds(0, n_cxy - 1)]
            pltpu.make_async_copy(gone, gone, send_sem.at[step, ROWS_C]).wait()


def body(observed, bucket, propensity, *state):
    rows, cols, delays = observed.shape
    part_a, rank = state[0].shape
    part_b = state[3].shape[0]
    n_camp, n_hour = lax.axis_size("camp"), lax.axis_size("hour")
    sizes = split_sizes(n_camp, n_hour)
    high, along_y, cores, along_x, low = sizes
    n_xy, n_z = along_x * along_y, high * low
    n_cxy, half, part_c = cores * n_xy, rank // cores, delays // n_xy
    scales = (
        1.0 / math.sqrt(cols * n_hour * delays),
        1.0 / math.sqrt(rows * n_camp * delays),
        1.0 / math.sqrt(rows * n_camp * cols * n_hour),
    )
    vmem = pltpu.VMEM
    scratch = [
        vmem((rows, cols, delays), bf16),
        vmem((rows, cols, delays), jnp.int32),
        vmem((rows, cols, delays), f32),
        pltpu.SMEM(propensity.shape, f32),
        vmem((propensity.shape[0], 8, delays), f32),
        vmem((rows, cols, delays), bf16),
    ]
    scratch += [vmem(s.shape, f32) for s in state]
    scratch += [vmem((STEPS, *p), bf16) for p in ((part_a, rank), (part_b, rank), (part_c, half))]
    scratch += [
        vmem((STEPS, n_hour, part_a, rank), bf16),
        vmem((STEPS, n_camp, part_b, rank), bf16),
        vmem((STEPS, n_cxy, part_c, half), bf16),
        vmem((1, n_cxy, part_c, half), f32),
        vmem((STEPS, n_hour, part_a, rank), bf16),
        vmem((STEPS, n_camp, part_b, rank), bf16),
        vmem((STEPS, n_cxy, part_c, half), bf16),
        vmem((STEPS, part_c, half), bf16),
        vmem((STEPS, n_hour, part_a, rank), bf16),
        vmem((STEPS, n_camp, part_b, rank), bf16),
        vmem((STEPS, n_cxy, part_c, half), bf16),
        vmem((STEPS, n_z, part_c, half), bf16),
        vmem((rows, rank), f32),
        vmem((cols, rank), bf16),
        vmem((cols, rank), f32),
        vmem((delays, rank), bf16),
        vmem((rank, delays), bf16),
        vmem((rows, 8, rank), f32),
        vmem((delays, rank), f32),
        pltpu.SemaphoreType.DMA((10,)),
        pltpu.SemaphoreType.DMA((2, CHUNKS)),
        pltpu.SemaphoreType.DMA((STEPS, KINDS)),
        pltpu.SemaphoreType.DMA((STEPS, KINDS)),
    ]
    def finish(*refs):
        copies = [pltpu.make_async_copy(refs[i], refs[3 + i], refs[6].at[i]) for i in range(3)]
        for c in copies:
            c.start()
        for c in copies:
            c.wait()

    anywhere, whole = pl.BlockSpec(memory_space=pltpu.HBM), pl.BlockSpec(memory_space=vmem)
    made = pl.pallas_call(
        functools.partial(kernel, sizes, scales),
        out_shape=(
            vmem(state[0].shape, f32),
            vmem(state[3].shape, f32),
            vmem(state[6].shape, f32),
        ),
        in_specs=[anywhere] * 12,
        out_specs=(whole, whole, whole),
        scratch_shapes=scratch,
        compiler_params=pltpu.CompilerParams(
            collective_id=0, has_side_effects=True, vmem_limit_bytes=40 * 1024 * 1024
        ),
        name="factor_steps",
    )(*[pltpu.with_memory_space_constraint(a, pltpu.HBM) for a in (observed, bucket, propensity, *state)])
    return pl.pallas_call(
        finish,
        out_shape=tuple(jax.ShapeDtypeStruct(m.shape, f32) for m in made),
        in_specs=[pl.BlockSpec(memory_space=vmem)] * 3,
        out_specs=(pl.BlockSpec(memory_space=pl.ANY),) * 3,
        scratch_shapes=[pltpu.SemaphoreType.DMA((3,))],
        name="outputs",
    )(*[pltpu.with_memory_space_constraint(m, vmem) for m in made])


def solution(mesh):
    rows_camp, rows_hour = P(("camp", "hour"), None), P(("hour", "camp"), None)
    in_specs = (
        P("camp", "hour", None),
        P("camp", "hour", None),
        P(),
        rows_camp,
        rows_camp,
        rows_camp,
        rows_hour,
        rows_hour,
        rows_hour,
        P(),
        P(),
        P(),
    )
    out_specs = (rows_camp, rows_hour, P())
    return jax.shard_map(body, mesh=mesh, in_specs=in_specs, out_specs=out_specs, check_vma=False)
```

```python
import functools
import math

import jax
import jax.numpy as jnp
from jax import lax
from jax.experimental import pallas as pl
from jax.experimental.pallas import tpu as pltpu
from jax.sharding import PartitionSpec as P

STEPS = 2

learn_rate = 0.1
beta_first = 0.9
beta_second = 0.999
adam_eps = 1e-08

MESH = pl.DeviceIdType.MESH
f32 = jnp.float32
bf16 = jnp.bfloat16

CHUNKS = 8
FIRST = 64
GROUP = 8
ALONG_Y = 2
ROWS_A, ROWS_B, ROWS_C, GRAD_A, GRAD_B, GRAD_C, SUM_C = range(7)
KINDS = 7


def split_sizes(camp_count, hour_count):
    high, core = 2, 2
    along_y = camp_count // (high * core)
    along_x = 4 if hour_count == 16 else 2
    return high, along_y, core, along_x, hour_count // along_x


def adam_update(factor, moment, second, gradient, grad_scale):
    scaled = gradient * grad_scale
    moment = beta_first * moment + (1.0 - beta_first) * scaled
    second = beta_second * second + (1.0 - beta_second) * scaled * scaled
    factor = factor - learn_rate * moment / (jnp.sqrt(second) + adam_eps)
    return factor, moment, second


def dot(a, b, dims):
    return lax.dot_general(a, b, (dims, ((), ())), preferred_element_type=f32)


def kernel(
    sizes,
    scales,
    obs_hbm,
    bucket_hbm,
    prop_hbm,
    *refs,
):
    state_hbm, refs = refs[:9], refs[9:]
    new_a, new_b, new_c, refs = *refs[:3], refs[3:]
    (
        obs,
        bucket,
        weight,
        prop,
        inverse,
        resid,
        fa,
        ma,
        va,
        fb,
        mb,
        vb,
        fc,
        mc,
        vc,
        a_own,
        b_own,
        c_own,
        a_all,
        b_all,
        c_all,
        c_last,
        ga_out,
        gb_out,
        gc_out,
        sc_out,
        ga_in,
        gb_in,
        gc_in,
        sc_in,
        a32,
        b16,
        b32,
        c16,
        ct16,
        ga8,
        gc,
        state_sem,
        chunk_sem,
        send_sem,
        recv_sem,
    ) = refs
    high, along_y, cores, along_x, low = sizes
    n_hour, n_camp = along_x * low, high * along_y * cores
    n_xy, n_z = along_x * along_y, high * low
    n_cxy, half = cores * n_xy, a32.shape[1] // cores
    scale_a, scale_b, scale_c = scales
    rows, cols, delays = obs.shape
    rank = a32.shape[1]
    part_b, part_c = cols // n_camp, delays // n_xy
    owners = ALONG_Y * cores
    width, y_blocks = owners * part_b, along_y // ALONG_Y

    camp, hour = lax.axis_index("camp"), lax.axis_index("hour")
    div, rem = lax.div, lax.rem
    z_hi, y, core = div(camp, along_y * cores), rem(div(camp, cores), along_y), rem(camp, cores)
    x, z_lo = div(hour, low), rem(hour, low)
    xy = x * along_y + y
    cxy, z = core * n_xy + xy, z_hi * low + z_lo

    def hour_peer(p):
        return {"camp": camp, "hour": p}

    def camp_peer(p):
        return {"camp": p, "hour": hour}

    def cxy_peer(p):
        at = rem(p, n_xy)
        return {"camp": (z_hi * along_y + rem(at, along_y)) * cores + div(p, n_xy), "hour": div(at, along_y) * low + z_lo}

    def z_peer(p):
        return {"camp": (div(p, low) * along_y + y) * cores + core, "hour": x * low + rem(p, low)}

    by_hour = (n_hour, hour, hour_peer)
    by_camp = (n_camp, camp, camp_peer)
    by_cxy = (n_cxy, cxy, cxy_peer)
    by_z = (n_z, z, z_peer)
    groups = (by_hour, by_camp, by_cxy, by_z)

    states = (fa, ma, va, fb, mb, vb, fc, mc, vc)
    loads = [pltpu.make_async_copy(h, v, state_sem.at[i]) for i, (h, v) in enumerate(zip(state_hbm, states))]
    loads.append(pltpu.make_async_copy(prop_hbm, prop, state_sem.at[9]))
    for load in loads:
        load.start()
    chunk = rows // CHUNKS

    def chunks_of(source, target, row):
        ats = [pl.ds(n * chunk, chunk) for n in range(CHUNKS)]
        return [pltpu.make_async_copy(source.at[at], target.at[at], chunk_sem.at[row, n]) for n, at in enumerate(ats)]

    bucket_chunks, obs_chunks = chunks_of(bucket_hbm, bucket, 0), chunks_of(obs_hbm, obs, 1)
    for load in bucket_chunks + obs_chunks:
        load.start()

    barrier = pltpu.get_barrier_semaphore()
    for size, me, peer in groups:
        for t in range(1, size):
            pl.semaphore_signal(barrier, inc=1, device_id=peer(rem(me + t, size)), device_id_type=MESH)
    pl.semaphore_wait(barrier, sum(size - 1 for size, _, _ in groups))

    def send(src, dst, step, kind, device):
        pltpu.make_async_remote_copy(
            src_ref=src,
            dst_ref=dst,
            send_sem=send_sem.at[step, kind],
            recv_sem=recv_sem.at[step, kind],
            device_id=device,
            device_id_type=MESH,
        ).start()

    def to_each(group, src, dst, step, kind):
        size, me, peer = group
        for t in range(1, size):
            p = rem(me + t, size)
            block = src.at[step] if len(src.shape) == len(dst.shape) - 1 else src.at[step, p]
            send(block, dst.at[step, me], step, kind, peer(p))

    def arrived(size, dst, step, kind):
        got = dst.at[step, pl.ds(0, size - 1)]
        pltpu.make_async_copy(got, got, recv_sem.at[step, kind]).wait()

    def total(buf, step, size):
        out = buf[step, 0].astype(f32)
        for p in range(1, size):
            out = out + buf[step, p].astype(f32)
        return out

    def give(own, everyone, group, value, step, kind):
        own[step] = value
        everyone[step, group[1]] = value
        to_each(group, own, everyone, step, kind)

    for load in loads:
        load.wait()
    give(a_own, a_all, by_hour, fa[...].astype(bf16), 0, ROWS_A)
    give(b_own, b_all, by_camp, fb[...].astype(bf16), 0, ROWS_B)

    for level in range(prop.shape[0]):
        inverse[level] = 1.0 / jnp.full((8, delays), prop[level], f32)

    def weigh(i, _):
        b = bucket[i].reshape(cols // 8, 8, delays)

        def inv(level):
            return jnp.broadcast_to(inverse[level][None], b.shape)

        one, two, four = (b & 1) != 0, (b & 2) != 0, (b & 4) != 0
        last = jnp.where(b > 7, inv(7), 0.0)
        low_half = jnp.where(two, jnp.where(one, inv(2), inv(1)), jnp.where(one, inv(0), last))
        high_half = jnp.where(two, jnp.where(one, inv(6), inv(5)), jnp.where(one, inv(4), inv(3)))
        weight[i] = jnp.where(four, high_half, low_half).reshape(cols, delays)
        return 0

    for n in range(CHUNKS):
        bucket_chunks[n].wait()
        lax.fori_loop(n * chunk, (n + 1) * chunk, weigh, 0)
    for load in obs_chunks:
        load.wait()

    c16[...] = fc[...].astype(bf16)
    c_mine = (pl.ds(pl.multiple_of(xy * part_c, 8), part_c), pl.ds(pl.multiple_of(core * half, 128), half))

    def halves(buf):
        return [(buf.at[pl.ds(n * n_xy, n_xy)], slice(n * half, (n + 1) * half)) for n in range(cores)]


    for step in range(STEPS):
        last = step == STEPS - 1
        ga8[...] = jnp.zeros_like(ga8)
        gc[...] = jnp.zeros_like(gc)
        arrived(n_hour, a_all, step, ROWS_A)
        arrived(n_camp, b_all, step, ROWS_B)
        a32[...] = a_all[step].astype(f32).reshape(rows, rank)
        b32[...] = b_all[step].astype(f32).reshape(cols, rank)
        b16[...] = b32[...].astype(bf16)
        if step > 0:
            arrived(n_cxy, c_all, step - 1, ROWS_C)
            for blocks, ranks in halves(c_all.at[step - 1]):
                c16[:, ranks] = blocks[...].astype(f32).reshape(delays, half).astype(bf16)
        ct16[...] = c16[...].astype(f32).T.astype(bf16)

        def first_pass(g, _):
            begin = g * FIRST
            pairs, residuals = [], []
            for i in range(0, FIRST, 2):
                at = pl.ds(begin + i, 2)
                pair = jnp.concatenate([a32[pl.ds(begin + i + u, 1), :].astype(bf16) * b16[...] for u in range(2)], 0)
                model = dot(pair, ct16[...], ((1,), (0,)))
                seen = obs[at].reshape(2 * cols, delays).astype(f32)
                residual = (weight[at].reshape(2 * cols, delays) * (model - seen)).astype(bf16)
                resid[at] = residual.reshape(2, cols, delays)
                pairs.append(pair)
                residuals.append(residual)
            gc[...] += dot(jnp.concatenate(residuals, 0), jnp.concatenate(pairs, 0), ((0,), (0,)))
            return 0

        lax.fori_loop(0, rows // FIRST, first_pass, 0)
        for blocks, ranks in halves(gc_out.at[step]):
            blocks[...] = gc[:, ranks].reshape(n_xy, part_c, half).astype(bf16)
        gc_in[step, cxy] = gc_out[step, cxy]
        to_each(by_cxy, gc_out, gc_in, step, GRAD_C)

        def second_pass(t, _):
            there = rem(z_hi + 1 + div(t, y_blocks), high) * y_blocks
            there += rem(div(y, ALONG_Y) + 1 + rem(t, y_blocks), y_blocks)
            cut = pl.multiple_of(there * width, width)
            at = pl.ds(cut, width)
            sums = [jnp.zeros((8, rank), f32) for _ in range(width // 8)]
            factor = b32[at]
            for begin in range(0, rows, GROUP):
                spread = dot(resid[pl.ds(begin, GROUP), at].reshape(GROUP * width, delays), c16[...], ((1,), (0,)))
                for u in range(GROUP):
                    row = a32[pl.ds(begin + u, 1), :]
                    part = None
                    for n in range(width // 8):
                        piece = spread[u * width + n * 8 : u * width + n * 8 + 8]
                        sums[n] = sums[n] + row * piece
                        scaled = factor[n * 8 : n * 8 + 8] * piece
                        part = scaled if part is None else part + scaled
                    ga8[begin + u] += part
            peer_rows = jnp.concatenate(sums, 0).reshape(owners, part_b, rank).astype(bf16)
            for n in range(owners):
                owner = there * owners + n

                @pl.when(owner != camp)
                def _(n=n, owner=owner):
                    gb_out[step, owner] = peer_rows[n]
                    send(gb_out.at[step, owner], gb_in.at[step, camp], step, GRAD_B, camp_peer(owner))

                @pl.when(owner == camp)
                def _(n=n, owner=owner):
                    gb_in[step, owner] = peer_rows[n]

            return 0

        lax.fori_loop(0, cols // width, second_pass, 0)
        ga_out[step] = jnp.sum(ga8[...], axis=1).reshape(ga_out.shape[1:]).astype(bf16)
        ga_in[step, hour] = ga_out[step, hour]
        to_each(by_hour, ga_out, ga_in, step, GRAD_A)

        arrived(n_cxy, gc_in, step, GRAD_C)
        give(sc_out, sc_in, by_z, total(gc_in, step, n_cxy).astype(bf16), step, SUM_C)

        arrived(n_camp, gb_in, step, GRAD_B)
        fb[...], mb[...], vb[...] = adam_update(fb[...], mb[...], vb[...], total(gb_in, step, n_camp), scale_b)
        if not last:
            give(b_own, b_all, by_camp, fb[...].astype(bf16), step + 1, ROWS_B)

        arrived(n_hour, ga_in, step, GRAD_A)
        fa[...], ma[...], va[...] = adam_update(fa[...], ma[...], va[...], total(ga_in, step, n_hour), scale_a)
        if not last:
            give(a_own, a_all, by_hour, fa[...].astype(bf16), step + 1, ROWS_A)

        arrived(n_z, sc_in, step, SUM_C)
        fresh = adam_update(fc[c_mine], mc[c_mine], vc[c_mine], total(sc_in, step, n_z), scale_c)
        fc[c_mine], mc[c_mine], vc[c_mine] = fresh
        if not last:
            give(c_own, c_all, by_cxy, fresh[0].astype(bf16), step, ROWS_C)
        else:
            c_last[0, cxy] = fresh[0]
            for t in range(1, n_cxy):
                send(c_last.at[0, cxy], c_last.at[0, cxy], step, ROWS_C, cxy_peer(rem(cxy + t, n_cxy)))
            new_a[...] = fa[...]
            new_b[...] = fb[...]
            got = c_last.at[0, pl.ds(0, n_cxy - 1)]
            pltpu.make_async_copy(got, got, recv_sem.at[step, ROWS_C]).wait()
            for blocks, ranks in halves(c_last.at[0]):
                new_c[:, ranks] = blocks[...].reshape(delays, half)

    def sent(size, buf, step, kind):
        gone = buf.at[step, pl.ds(0, size - 1)]
        pltpu.make_async_copy(gone, gone, send_sem.at[step, kind]).wait()

    for step in range(STEPS):
        sent(n_hour, a_all, step, ROWS_A)
        sent(n_camp, b_all, step, ROWS_B)
        sent(n_hour, ga_in, step, GRAD_A)
        sent(n_camp, gb_in, step, GRAD_B)
        sent(n_cxy, gc_in, step, GRAD_C)
        sent(n_z, sc_in, step, SUM_C)
        if step < STEPS - 1:
            sent(n_cxy, c_all, step, ROWS_C)
        else:
            gone = c_last.at[0, pl.ds(0, n_cxy - 1)]
            pltpu.make_async_copy(gone, gone, send_sem.at[step, ROWS_C]).wait()


def body(observed, bucket, propensity, *state):
    rows, cols, delays = observed.shape
    part_a, rank = state[0].shape
    part_b = state[3].shape[0]
    n_camp, n_hour = lax.axis_size("camp"), lax.axis_size("hour")
    sizes = split_sizes(n_camp, n_hour)
    high, along_y, cores, along_x, low = sizes
    n_xy, n_z = along_x * along_y, high * low
    n_cxy, half, part_c = cores * n_xy, rank // cores, delays // n_xy
    scales = (
        1.0 / math.sqrt(cols * n_hour * delays),
        1.0 / math.sqrt(rows * n_camp * delays),
        1.0 / math.sqrt(rows * n_camp * cols * n_hour),
    )
    vmem = pltpu.VMEM
    scratch = [
        vmem((rows, cols, delays), bf16),
        vmem((rows, cols, delays), jnp.int32),
        vmem((rows, cols, delays), f32),
        pltpu.SMEM(propensity.shape, f32),
        vmem((propensity.shape[0], 8, delays), f32),
        vmem((rows, cols, delays), bf16),
    ]
    scratch += [vmem(s.shape, f32) for s in state]
    scratch += [vmem((STEPS, *p), bf16) for p in ((part_a, rank), (part_b, rank), (part_c, half))]
    scratch += [
        vmem((STEPS, n_hour, part_a, rank), bf16),
        vmem((STEPS, n_camp, part_b, rank), bf16),
        vmem((STEPS, n_cxy, part_c, half), bf16),
        vmem((1, n_cxy, part_c, half), f32),
        vmem((STEPS, n_hour, part_a, rank), bf16),
        vmem((STEPS, n_camp, part_b, rank), bf16),
        vmem((STEPS, n_cxy, part_c, half), bf16),
        vmem((STEPS, part_c, half), bf16),
        vmem((STEPS, n_hour, part_a, rank), bf16),
        vmem((STEPS, n_camp, part_b, rank), bf16),
        vmem((STEPS, n_cxy, part_c, half), bf16),
        vmem((STEPS, n_z, part_c, half), bf16),
        vmem((rows, rank), f32),
        vmem((cols, rank), bf16),
        vmem((cols, rank), f32),
        vmem((delays, rank), bf16),
        vmem((rank, delays), bf16),
        vmem((rows, 8, rank), f32),
        vmem((delays, rank), f32),
        pltpu.SemaphoreType.DMA((10,)),
        pltpu.SemaphoreType.DMA((2, CHUNKS)),
        pltpu.SemaphoreType.DMA((STEPS, KINDS)),
        pltpu.SemaphoreType.DMA((STEPS, KINDS)),
    ]
    def finish(*refs):
        copies = [pltpu.make_async_copy(refs[i], refs[3 + i], refs[6].at[i]) for i in range(3)]
        for c in copies:
            c.start()
        for c in copies:
            c.wait()

    anywhere, whole = pl.BlockSpec(memory_space=pltpu.HBM), pl.BlockSpec(memory_space=vmem)
    made = pl.pallas_call(
        functools.partial(kernel, sizes, scales),
        out_shape=(
            vmem(state[0].shape, f32),
            vmem(state[3].shape, f32),
            vmem(state[6].shape, f32),
        ),
        in_specs=[anywhere] * 12,
        out_specs=(whole, whole, whole),
        scratch_shapes=scratch,
        compiler_params=pltpu.CompilerParams(
            collective_id=0, has_side_effects=True, vmem_limit_bytes=40 * 1024 * 1024
        ),
        name="factor_steps",
    )(*[pltpu.with_memory_space_constraint(a, pltpu.HBM) for a in (observed, bucket, propensity, *state)])
    return pl.pallas_call(
        finish,
        out_shape=tuple(jax.ShapeDtypeStruct(m.shape, f32) for m in made),
        in_specs=[pl.BlockSpec(memory_space=vmem)] * 3,
        out_specs=(pl.BlockSpec(memory_space=pl.ANY),) * 3,
        scratch_shapes=[pltpu.SemaphoreType.DMA((3,))],
        name="outputs",
    )(*[pltpu.with_memory_space_constraint(m, vmem) for m in made])


def solution(mesh):
    rows_camp, rows_hour = P(("camp", "hour"), None), P(("hour", "camp"), None)
    in_specs = (
        P("camp", "hour", None),
        P("camp", "hour", None),
        P(),
        rows_camp,
        rows_camp,
        rows_camp,
        rows_hour,
        rows_hour,
        rows_hour,
        P(),
        P(),
        P(),
    )
    out_specs = (rows_camp, rows_hour, P())
    return jax.shard_map(body, mesh=mesh, in_specs=in_specs, out_specs=out_specs, check_vma=False)
```
